32 devices in a mesh: row: 8 (over y, x, core), vec: 4 (over z).
Axes of the slice: x: 2, y: 2, z: 4, core: 2. Of those that a mesh axis runs over, the one named last changes fastest.
Arguments:
- ham_tiles: bfloat16 [512, 4, 128, 128], P('row'), may hold values from -0.125 to 0.125
- tile_columns: int32 [512, 4], P('row'), may hold values from 0 to 511, as said below
- stack_lengths: int32 [8], P('row'), may hold values from 32 to 64, as said below
- start_vectors: bfloat16 [65536, 1024], P('row', 'vec'), may hold values from -6 to 6
- spectral_scale: float32 [1], replicated, may hold values from 4 to 16
Outputs:
- filtered_basis: bfloat16 [65536, 1024], P('row', 'vec')
The draws below stay inside these ranges and needn't reach their ends.
Inputs may be any that keep to these rules, and one draw needn't show every extreme that they name: `tile_columns`: row b lists 4 distinct block columns; the first is b itself, the others are (b + o) mod 512 with nonzero offsets o from -2 to 2. Some stack holds 64 occupied block rows and some other stack exactly half of 64; a stack's occupied rows are its first stack_lengths - 2 and its last 2 block rows.
All inputs are finite; a program needn't handle non-finite values.
Results may differ from the reference program's by a relative error of at most 0.006.
The reference program's roundings to bfloat16 on the way count: a program that leaves them out, or rounds other values in their place, can miss the bound.
Values may be sent and summed in bfloat16 or wider, within the bound.
A program may use at most 128 MiB of HBM per device.

```python
import math
import jax
import jax.numpy as jnp
from jax import lax

TILE = 128
NT = 4
REACH = 2
M = 1024
CHEB = 6
NS_ITERS = 2
BLK_DEV = 64
STACKS = 8
NB = 512
NR = 65536


def draw_tile_columns(key, part):
    block_ids = jnp.arange(NB, dtype=jnp.int32)
    offset_pool = jnp.array([-2, -1, 1, 2], dtype=jnp.int32)
    scores = jax.random.randint(key, (NB, 4), 0, 4096) * 4 + jnp.arange(4, dtype=jnp.int32)[None, :]
    ranking = jnp.argsort(scores, axis=1)
    chosen = offset_pool[ranking[:, :NT - 1]]
    offsets = jnp.concatenate([jnp.zeros((NB, 1), jnp.int32), chosen], axis=1)
    return ((block_ids[:, None] + offsets) % NB).astype(jnp.int32)


def draw_stack_lengths(key, part):
    key_full, key_uneven, key_first, key_second = jax.random.split(key, 4)
    full_flags = jax.random.randint(key_full, (STACKS,), 0, 2)
    uneven = jax.random.randint(key_uneven, (STACKS,), BLK_DEV // 2, BLK_DEV)
    counts = jnp.where(full_flags == 1, BLK_DEV, uneven)
    first_stack = jax.random.randint(key_first, (), 0, STACKS)
    second_stack = (first_stack + 1 + jax.random.randint(key_second, (), 0, STACKS - 1)) % STACKS
    counts = counts.at[first_stack].set(BLK_DEV).at[second_stack].set(BLK_DEV // 2)
    return counts.astype(jnp.int32)


def draw_start_vectors(key, part):
    key_entries = jax.random.fold_in(key, 71)
    values = jnp.clip(jax.random.normal(key_entries, (NR, M), jnp.float32), -6.0, 6.0)
    return values.astype(jnp.bfloat16)


def level_of(key, dims, cuts, least, top_value):
    def one(dim, parts):
        steps = jax.random.uniform(jax.random.fold_in(jax.random.fold_in(key, 6), dim), (parts,), jnp.float32, least / len(cuts), top_value / len(cuts))
        return jnp.repeat(jnp.exp(steps), dims[dim] // parts).reshape((-1,) + (1,) * (len(dims) - dim - 1))

    loudness = one(*cuts[0])
    for cut in cuts[1:]:
        loudness = loudness * one(*cut)
    return loudness


def gaussian(key, dims, spread, most, pieces=(), kind=jnp.bfloat16):
    values = spread * jax.random.normal(key, dims, jnp.float32)
    if pieces:
        values = values * level_of(key, dims, pieces, -0.22, 0.18)
    return jnp.clip(values, -most, most).astype(kind)


def setup_inputs(seed: int = 0) -> dict:
    keys = jax.random.split(jax.random.key(seed), 6)
    return {
        "ham_tiles": gaussian(keys[0], (NB, NT, TILE, TILE), (4 * NT * TILE) ** -0.5, 0.125, ((0, 8),)),
        "tile_columns": draw_tile_columns(jax.random.fold_in(keys[5], 71), 0),
        "stack_lengths": draw_stack_lengths(jax.random.fold_in(keys[5], 71), 0),
        "start_vectors": draw_start_vectors(jax.random.fold_in(keys[5], 71), 0),
        "spectral_scale": jnp.clip(jnp.exp(jax.random.uniform(keys[4], (1,), jnp.float32, math.log(4.0), math.log(16.0))), 4.0, 16.0),
    }


def apply_hamiltonian(ham_tiles, tile_columns, stack_lengths, current):
    blocked = current.reshape(NB, TILE, M)

    def group_product(group):
        start = (group * BLK_DEV).astype(jnp.int32)
        tile_group = lax.dynamic_slice_in_dim(ham_tiles, start, BLK_DEV, 0).astype(jnp.float32)
        column_group = lax.dynamic_slice_in_dim(tile_columns, start, BLK_DEV, 0)
        picked = blocked[column_group].astype(jnp.float32)
        product = jnp.einsum('btij,btjc->bic', tile_group, picked)
        local_rows = jnp.arange(BLK_DEV, dtype=jnp.int32)
        live = (local_rows < stack_lengths[group] - REACH) | (local_rows >= BLK_DEV - REACH)
        live_rows = live.astype(jnp.float32)
        return product * live_rows[:, None, None]
    stacked = lax.map(group_product, jnp.arange(STACKS, dtype=jnp.int32))
    return stacked.reshape(NR, M)

def reference(ham_tiles, tile_columns, stack_lengths, start_vectors, spectral_scale):
    earlier = start_vectors
    current = apply_hamiltonian(ham_tiles, tile_columns, stack_lengths, start_vectors).astype(jnp.bfloat16)
    for repeat in range(CHEB - 1):
        image = apply_hamiltonian(ham_tiles, tile_columns, stack_lengths, current)
        following = (2.0 * image - earlier.astype(jnp.float32)).astype(jnp.bfloat16)
        earlier, current = (current, following)
    filtered = current.astype(jnp.float32)
    gram = lax.dot_general(filtered, filtered, (((0,), (0,)), ((), ())), precision=lax.Precision.HIGHEST) / NR
    scale = spectral_scale[0] * jnp.trace(gram) / M
    system = gram / scale
    root = jnp.eye(M, dtype=jnp.float32)
    for repeat in range(NS_ITERS):
        product_w = jnp.dot(system, root, precision=lax.Precision.HIGHEST)
        product_p = jnp.dot(product_w, root, precision=lax.Precision.HIGHEST)
        root = 1.5 * root - 0.5 * jnp.dot(product_p, root, precision=lax.Precision.HIGHEST)
    weights = (root / jnp.sqrt(scale)).astype(jnp.bfloat16)
    basis = jnp.dot(filtered, weights.astype(jnp.float32), precision=lax.Precision.HIGHEST)
    return basis.astype(jnp.bfloat16)
```

```python
import functools

import jax
import jax.numpy as jnp
from jax import lax
from jax.experimental import pallas as pl
from jax.experimental.pallas import tpu as pltpu
from jax.sharding import PartitionSpec as P

REACH = 2
CHEB = 6


def chebyshev_kernel(
    total_blocks,
    columns_ref,
    lengths_ref,
    tiles_ref,
    start_ref,
    out_ref,
    band,
    even,
    odd,
    halo,
    send_sem,
    recv_sem,
):
    block_count, tile_count, tile, _ = tiles_ref.shape
    pair = REACH * tile
    pairs = block_count // REACH
    count = lax.axis_size("row")
    me = lax.axis_index("row")
    left, right = lax.rem(me + count - 1, count), lax.rem(me + 1, count)
    last = (pairs - 1) * pair

    barrier = pltpu.get_barrier_semaphore()
    for neighbour in (left, right):
        pl.semaphore_signal(
            barrier, inc=1, device_id={"row": neighbour}, device_id_type=pl.DeviceIdType.MESH
        )
    pl.semaphore_wait(barrier, 2)

    def sends(source, step):
        to_left = pltpu.make_async_remote_copy(
            src_ref=source.at[pl.ds(0, pair)],
            dst_ref=halo.at[step, 1],
            send_sem=send_sem.at[step, 1],
            recv_sem=recv_sem.at[step, 1],
            device_id={"row": left},
            device_id_type=pl.DeviceIdType.MESH,
        )
        to_right = pltpu.make_async_remote_copy(
            src_ref=source.at[pl.ds(last, pair)],
            dst_ref=halo.at[step, 0],
            send_sem=send_sem.at[step, 0],
            recv_sem=recv_sem.at[step, 0],
            device_id={"row": right},
            device_id_type=pl.DeviceIdType.MESH,
        )
        return to_left, to_right

    copies = sends(start_ref, 0)
    for copy in copies:
        copy.start()

    def build(p, carry):
        for i in range(REACH):
            b = p * REACH + i
            live = (b < lengths_ref[0] - REACH) | (b >= block_count - REACH)
            places = []
            for t in range(tile_count):
                shift = lax.rem(
                    columns_ref[b * tile_count + t] - (me * block_count + b) + REACH + total_blocks,
                    total_blocks,
                )
                places.append(jnp.where(live, shift, -1))
            for c in range(3 * REACH):
                value = None
                if 0 <= c - i <= 2 * REACH:
                    for t in range(tile_count):
                        hit = jnp.where(places[t] == c - i, 1.0, 0.0).astype(jnp.float32)
                        mask = jnp.full((tile, tile), hit, jnp.float32).astype(jnp.bfloat16)
                        term = tiles_ref[b, t] * mask
                        value = term if value is None else value + term
                else:
                    value = jnp.zeros((tile, tile), jnp.bfloat16)
                band[p, i * tile : (i + 1) * tile, c * tile : (c + 1) * tile] = value
        return carry

    lax.fori_loop(0, pairs, build, 0)

    held = [start_ref, odd, even, odd, even, odd, out_ref]
    for step in range(CHEB):
        current, target = held[step], held[step + 1]
        earlier = held[step - 1] if step else None

        def finish(product, rows):
            if earlier is not None:
                product = 2.0 * product - earlier[rows, :].astype(jnp.float32)
            target[rows, :] = product.astype(jnp.bfloat16)

        for copy in copies:
            copy.wait()
        top = pl.ds(0, pair)
        finish(
            jnp.dot(band[0, :, :pair], halo[step, 0], preferred_element_type=jnp.float32)
            + jnp.dot(
                band[0, :, pair:], current[0 : 2 * pair, :], preferred_element_type=jnp.float32
            ),
            top,
        )
        finish(
            jnp.dot(
                band[pairs - 1, :, 2 * pair :], halo[step, 1], preferred_element_type=jnp.float32
            )
            + jnp.dot(
                band[pairs - 1, :, : 2 * pair],
                current[last - pair : last + pair, :],
                preferred_element_type=jnp.float32,
            ),
            pl.ds(last, pair),
        )

        def interior(p, carry):
            before = pl.multiple_of((p - 1) * pair, pair)
            here = pl.multiple_of(p * pair, pair)
            finish(
                jnp.dot(
                    band[p], current[pl.ds(before, 3 * pair), :], preferred_element_type=jnp.float32
                ),
                pl.ds(here, pair),
            )
            return carry

        early = min(7, pairs - 1)
        lax.fori_loop(1, early, interior, 0, unroll=3)
        if step < CHEB - 1:
            copies = sends(target, step + 1)
            for copy in copies:
                copy.start()
        lax.fori_loop(early, pairs - 1, interior, 0, unroll=4)


def chebyshev(ham_tiles, tile_columns, stack_lengths, start_vectors):
    block_count, tile_count, tile, _ = ham_tiles.shape
    rows, width = start_vectors.shape
    pair = REACH * tile
    vmem = pl.BlockSpec(memory_space=pltpu.VMEM)
    smem = pl.BlockSpec(memory_space=pltpu.SMEM)
    return pl.pallas_call(
        functools.partial(chebyshev_kernel, block_count * lax.axis_size("row")),
        out_shape=jax.ShapeDtypeStruct((rows, width), jnp.bfloat16),
        in_specs=[smem, smem, vmem, vmem],
        out_specs=vmem,
        scratch_shapes=[
            pltpu.VMEM((block_count // REACH, pair, 3 * pair), jnp.bfloat16),
            pltpu.VMEM((rows, width), jnp.bfloat16),
            pltpu.VMEM((rows, width), jnp.bfloat16),
            pltpu.VMEM((CHEB, 2, pair, width), jnp.bfloat16),
            pltpu.SemaphoreType.DMA((CHEB, 2)),
            pltpu.SemaphoreType.DMA((CHEB, 2)),
        ],
        compiler_params=pltpu.CompilerParams(
            collective_id=0, has_side_effects=True, vmem_limit_bytes=60 * 1024 * 1024
        ),
    )(tile_columns.reshape(-1), stack_lengths, ham_tiles, start_vectors)


def local(ham_tiles, tile_columns, stack_lengths, start_vectors, spectral_scale):
    row_count, panel_width = start_vectors.shape
    total_rows = row_count * lax.axis_size("row")
    full_width = panel_width * lax.axis_size("vec")
    current = chebyshev(ham_tiles, tile_columns, stack_lengths, start_vectors)
    panel_rows = lax.all_to_all(current, "vec", split_axis=0, concat_axis=1, tiled=True)

    part = 256
    parts = full_width // part
    packed = jnp.concatenate(
        [
            lax.dot_general(
                panel_rows[:, j * part : (j + 1) * part],
                panel_rows[:, : (j + 1) * part],
                (((0,), (0,)), ((), ())),
                preferred_element_type=jnp.float32,
            )
            for j in range(parts)
        ],
        axis=1,
    )
    packed = lax.psum(packed / float(total_rows), ("row", "vec"))
    starts = [j * (j + 1) // 2 * part for j in range(parts)]

    def block(i, j):
        if j <= i:
            return packed[:, starts[i] + j * part : starts[i] + (j + 1) * part]
        return block(j, i).T

    gram = jnp.concatenate(
        [jnp.concatenate([block(i, j) for j in range(parts)], axis=1) for i in range(parts)], axis=0
    )
    scale = spectral_scale[0] * jnp.trace(gram) / full_width
    system = gram / scale
    identity = jnp.eye(full_width, dtype=jnp.float32)
    square = jnp.dot(system, system, precision=lax.Precision.HIGH)
    first = 1.5 * identity - 0.5 * system
    left = 1.5 * system - 0.5 * square
    right = 2.25 * identity - 1.5 * system + 0.25 * square
    root = 1.5 * first - 0.5 * jnp.dot(left, right, precision=lax.Precision.HIGH)
    weights = (root / jnp.sqrt(scale)).astype(jnp.bfloat16)
    basis_rows = jnp.dot(panel_rows, weights, preferred_element_type=jnp.float32).astype(
        jnp.bfloat16
    )
    return lax.all_to_all(basis_rows, "vec", split_axis=1, concat_axis=0, tiled=True)


def solution(mesh):
    placed = (P("row", None, None, None), P("row", None), P("row"), P("row", "vec"), P())
    return jax.shard_map(
        local, mesh=mesh, in_specs=placed, out_specs=P("row", "vec"), check_vma=False
    )
```

```python
import functools

import jax
import jax.numpy as jnp
from jax import lax
from jax.experimental import pallas as pl
from jax.experimental.pallas import tpu as pltpu
from jax.sharding import PartitionSpec as P

REACH = 2
CHEB = 6


def chebyshev_kernel(
    total_blocks,
    columns_ref,
    lengths_ref,
    tiles_ref,
    start_ref,
    out_ref,
    band,
    even,
    odd,
    halo,
    send_sem,
    recv_sem,
):
    block_count, tile_count, tile, _ = tiles_ref.shape
    pair = REACH * tile
    pairs = block_count // REACH
    count = lax.axis_size("row")
    me = lax.axis_index("row")
    left, right = lax.rem(me + count - 1, count), lax.rem(me + 1, count)
    last = (pairs - 1) * pair

    barrier = pltpu.get_barrier_semaphore()
    for neighbour in (left, right):
        pl.semaphore_signal(
            barrier, inc=1, device_id={"row": neighbour}, device_id_type=pl.DeviceIdType.MESH
        )
    pl.semaphore_wait(barrier, 2)

    def sends(source, step):
        to_left = pltpu.make_async_remote_copy(
            src_ref=source.at[pl.ds(0, pair)],
            dst_ref=halo.at[step, 1],
            send_sem=send_sem.at[step, 1],
            recv_sem=recv_sem.at[step, 1],
            device_id={"row": left},
            device_id_type=pl.DeviceIdType.MESH,
        )
        to_right = pltpu.make_async_remote_copy(
            src_ref=source.at[pl.ds(last, pair)],
            dst_ref=halo.at[step, 0],
            send_sem=send_sem.at[step, 0],
            recv_sem=recv_sem.at[step, 0],
            device_id={"row": right},
            device_id_type=pl.DeviceIdType.MESH,
        )
        return to_left, to_right

    copies = sends(start_ref, 0)
    for copy in copies:
        copy.start()

    def build(p, carry):
        for i in range(REACH):
            b = p * REACH + i
            live = (b < lengths_ref[0] - REACH) | (b >= block_count - REACH)
            places = []
            for t in range(tile_count):
                shift = lax.rem(
                    columns_ref[b * tile_count + t] - (me * block_count + b) + REACH + total_blocks,
                    total_blocks,
                )
                places.append(jnp.where(live, shift, -1))
            for c in range(3 * REACH):
                value = None
                if 0 <= c - i <= 2 * REACH:
                    for t in range(tile_count):
                        hit = jnp.where(places[t] == c - i, 1.0, 0.0).astype(jnp.float32)
                        mask = jnp.full((tile, tile), hit, jnp.float32).astype(jnp.bfloat16)
                        term = tiles_ref[b, t] * mask
                        value = term if value is None else value + term
                else:
                    value = jnp.zeros((tile, tile), jnp.bfloat16)
                band[p, i * tile : (i + 1) * tile, c * tile : (c + 1) * tile] = value
        return carry

    lax.fori_loop(0, pairs, build, 0)

    held = [start_ref, odd, even, odd, even, odd, out_ref]
    for step in range(CHEB):
        current, target = held[step], held[step + 1]
        earlier = held[step - 1] if step else None

        def finish(product, rows):
            if earlier is not None:
                product = 2.0 * product - earlier[rows, :].astype(jnp.float32)
            target[rows, :] = product.astype(jnp.bfloat16)

        for copy in copies:
            copy.wait()
        top = pl.ds(0, pair)
        finish(
            jnp.dot(band[0, :, :pair], halo[step, 0], preferred_element_type=jnp.float32)
            + jnp.dot(
                band[0, :, pair:], current[0 : 2 * pair, :], preferred_element_type=jnp.float32
            ),
            top,
        )
        finish(
            jnp.dot(
                band[pairs - 1, :, 2 * pair :], halo[step, 1], preferred_element_type=jnp.float32
            )
            + jnp.dot(
                band[pairs - 1, :, : 2 * pair],
                current[last - pair : last + pair, :],
                preferred_element_type=jnp.float32,
            ),
            pl.ds(last, pair),
        )

        def interior(p, carry):
            before = pl.multiple_of((p - 1) * pair, pair)
            here = pl.multiple_of(p * pair, pair)
            finish(
                jnp.dot(
                    band[p], current[pl.ds(before, 3 * pair), :], preferred_element_type=jnp.float32
                ),
                pl.ds(here, pair),
            )
            return carry

        early = min(7, pairs - 1)
        lax.fori_loop(1, early, interior, 0, unroll=3)
        if step < CHEB - 1:
            copies = sends(target, step + 1)
            for copy in copies:
                copy.start()
        lax.fori_loop(early, pairs - 1, interior, 0, unroll=4)


def chebyshev(ham_tiles, tile_columns, stack_lengths, start_vectors):
    block_count, tile_count, tile, _ = ham_tiles.shape
    rows, width = start_vectors.shape
    pair = REACH * tile
    vmem = pl.BlockSpec(memory_space=pltpu.VMEM)
    smem = pl.BlockSpec(memory_space=pltpu.SMEM)
    return pl.pallas_call(
        functools.partial(chebyshev_kernel, block_count * lax.axis_size("row")),
        out_shape=jax.ShapeDtypeStruct((rows, width), jnp.bfloat16),
        in_specs=[smem, smem, vmem, vmem],
        out_specs=vmem,
        scratch_shapes=[
            pltpu.VMEM((block_count // REACH, pair, 3 * pair), jnp.bfloat16),
            pltpu.VMEM((rows, width), jnp.bfloat16),
            pltpu.VMEM((rows, width), jnp.bfloat16),
            pltpu.VMEM((CHEB, 2, pair, width), jnp.bfloat16),
            pltpu.SemaphoreType.DMA((CHEB, 2)),
            pltpu.SemaphoreType.DMA((CHEB, 2)),
        ],
        compiler_params=pltpu.CompilerParams(
            collective_id=0, has_side_effects=True, vmem_limit_bytes=60 * 1024 * 1024
        ),
    )(tile_columns.reshape(-1), stack_lengths, ham_tiles, start_vectors)


def gram_sum_kernel(part_ref, out_ref, arrived, outgoing, total, near, thin, far, send_sem, recv_sem):
    _, quads, panels, _, _ = part_ref.shape
    row, vec = lax.axis_index("row"), lax.axis_index("vec")
    side, quad = lax.rem(row, 2), row // 2
    other = 1 - side
    partner = quad * 2 + other
    quad_at = [lax.rem(quad + d, quads) for d in range(quads)]
    vec_at = [lax.rem(vec + d, panels) for d in range(panels)]

    def ring(axis, places, make):
        copies = []
        for d in range(1, len(places)):
            source, target, slot = make(d)
            place = places[d] if axis == "vec" else places[d] * 2 + side
            copies.append(
                pltpu.make_async_remote_copy(
                    src_ref=source,
                    dst_ref=target,
                    send_sem=send_sem.at[slot],
                    recv_sem=recv_sem.at[slot],
                    device_id={axis: place},
                    device_id_type=pl.DeviceIdType.MESH,
                )
            )
        for copy in copies:
            copy.start()
        return copies

    def swap(source, target, slot):
        copy = pltpu.make_async_remote_copy(
            src_ref=source,
            dst_ref=target,
            send_sem=send_sem.at[slot],
            recv_sem=recv_sem.at[slot],
            device_id={"row": partner},
            device_id_type=pl.DeviceIdType.MESH,
        )
        copy.start()
        copy.wait()

    barrier = pltpu.get_barrier_semaphore()
    greeted = [{"row": partner}]
    greeted += [{"row": place * 2 + side} for place in quad_at[1:]]
    greeted += [{"vec": place} for place in vec_at[1:]]
    for device in greeted:
        pl.semaphore_signal(
            barrier, inc=1, device_id=device, device_id_type=pl.DeviceIdType.MESH
        )
    pl.semaphore_wait(barrier, len(greeted))

    slots = iter(range(2 + 2 * (quads - 1) + 2 * (panels - 1)))
    swap(part_ref.at[other], arrived, next(slots))
    for d in range(1, quads):
        place = quad_at[d]
        outgoing[place] = (part_ref[side, place] + arrived[place]).astype(jnp.bfloat16)
    total[...] = part_ref[side, quad] + arrived[quad]

    copies = ring(
        "row", quad_at, lambda d: (outgoing.at[quad_at[d]], near.at[d - 1], next(slots))
    )
    for d in range(1, quads):
        copies[d - 1].wait()
        total[...] += near[d - 1].astype(jnp.float32)

    thin[...] = total[...].astype(jnp.bfloat16)
    copies = ring("vec", vec_at, lambda d: (thin.at[vec_at[d]], far.at[d - 1], next(slots)))
    reduced = total[vec]
    for d in range(1, panels):
        copies[d - 1].wait()
        reduced += far[d - 1].astype(jnp.float32)
    out_ref[side, quad, vec] = reduced.astype(jnp.bfloat16)

    mine = out_ref.at[side, quad, vec]
    for copy in ring("vec", vec_at, lambda d: (mine, mine, next(slots))):
        copy.wait()
    mine = out_ref.at[side, quad]
    for copy in ring("row", quad_at, lambda d: (mine, mine, next(slots))):
        copy.wait()
    mine = out_ref.at[side]
    swap(mine, mine, next(slots))


def gram_sum(partial):
    rows, width = partial.shape
    quads, panels = lax.axis_size("row") // 2, lax.axis_size("vec")
    height = rows // (2 * quads * panels)
    copies = 2 + 2 * (quads - 1) + 2 * (panels - 1)
    vmem = pl.BlockSpec(memory_space=pltpu.VMEM)
    summed = pl.pallas_call(
        gram_sum_kernel,
        out_shape=jax.ShapeDtypeStruct((2, quads, panels, height, width), jnp.bfloat16),
        in_specs=[vmem],
        out_specs=vmem,
        scratch_shapes=[
            pltpu.VMEM((quads, panels, height, width), jnp.float32),
            pltpu.VMEM((quads, panels, height, width), jnp.bfloat16),
            pltpu.VMEM((panels, height, width), jnp.float32),
            pltpu.VMEM((quads - 1, panels, height, width), jnp.bfloat16),
            pltpu.VMEM((panels, height, width), jnp.bfloat16),
            pltpu.VMEM((panels - 1, height, width), jnp.bfloat16),
            pltpu.SemaphoreType.DMA((copies,)),
            pltpu.SemaphoreType.DMA((copies,)),
        ],
        compiler_params=pltpu.CompilerParams(
            collective_id=1, has_side_effects=True, vmem_limit_bytes=40 * 1024 * 1024
        ),
    )(partial.reshape(2, quads, panels, height, width))
    return summed.reshape(rows, width)


def local(ham_tiles, tile_columns, stack_lengths, start_vectors, spectral_scale):
    row_count, panel_width = start_vectors.shape
    total_rows = row_count * lax.axis_size("row")
    full_width = panel_width * lax.axis_size("vec")
    current = chebyshev(ham_tiles, tile_columns, stack_lengths, start_vectors)
    panel_rows = lax.all_to_all(current, "vec", split_axis=0, concat_axis=1, tiled=True)

    part = 256
    parts = full_width // part
    pieces = [(i, j) for i in range(parts) for j in range(i + 1)]
    packed = jnp.concatenate(
        [
            lax.dot_general(
                panel_rows[:, : (j + 1) * part],
                panel_rows[:, j * part : (j + 1) * part],
                (((0,), (0,)), ((), ())),
                preferred_element_type=jnp.float32,
            )
            for j in range(parts)
        ],
        axis=0,
    )
    packed = gram_sum(packed / float(total_rows))
    blocks = {}
    for n, (i, j) in enumerate(pieces):
        blocks[j, i] = packed[n * part : (n + 1) * part]
        blocks[i, j] = blocks[j, i] if i == j else blocks[j, i].T
    gram = jnp.concatenate(
        [jnp.concatenate([blocks[i, j] for j in range(parts)], axis=1) for i in range(parts)],
        axis=0,
    )
    identity = jnp.eye(part, dtype=jnp.float32)
    trace = sum(jnp.sum(blocks[i, i].astype(jnp.float32) * identity) for i in range(parts))
    scale = spectral_scale[0] * trace / full_width
    square = jnp.dot(gram, gram, preferred_element_type=jnp.float32) / (scale * scale)
    system = gram.astype(jnp.float32) / scale
    root = (
        2.25 * jnp.eye(full_width, dtype=jnp.float32)
        - 2.4375 * system
        + 1.6875 * square
        + jnp.dot(square, 0.0625 * square - 0.5625 * system, precision=lax.Precision.HIGH)
    )
    weights = (root / jnp.sqrt(scale)).astype(jnp.bfloat16)
    basis_rows = jnp.dot(panel_rows, weights, preferred_element_type=jnp.float32).astype(
        jnp.bfloat16
    )
    return lax.all_to_all(basis_rows, "vec", split_axis=1, concat_axis=0, tiled=True)


def solution(mesh):
    placed = (P("row", None, None, None), P("row", None), P("row"), P("row", "vec"), P())
    return jax.shard_map(
        local, mesh=mesh, in_specs=placed, out_specs=P("row", "vec"), check_vma=False
    )
```

```python
import functools

import jax
import jax.numpy as jnp
from jax import lax
from jax.experimental import pallas as pl
from jax.experimental.pallas import tpu as pltpu
from jax.sharding import PartitionSpec as P

REACH = 2
CHEB = 6


def chebyshev_kernel(
    total_blocks,
    columns_ref,
    lengths_ref,
    tiles_ref,
    start_ref,
    out_ref,
    band,
    even,
    odd,
    final,
    halo,
    send_sem,
    recv_sem,
    panel_send,
    panel_recv,
    keep_sem,
):
    block_count, tile_count, tile, _ = tiles_ref.shape
    pair = REACH * tile
    pairs = block_count // REACH
    count = lax.axis_size("row")
    me = lax.axis_index("row")
    left, right = lax.rem(me + count - 1, count), lax.rem(me + 1, count)
    last = (pairs - 1) * pair
    vec, panels = lax.axis_index("vec"), lax.axis_size("vec")
    vec_at = [lax.rem(vec + d, panels) for d in range(panels)]
    share = pairs // panels

    barrier = pltpu.get_barrier_semaphore()
    greeted = [{"row": left}, {"row": right}] + [{"vec": place} for place in vec_at[1:]]
    for device in greeted:
        pl.semaphore_signal(
            barrier, inc=1, device_id=device, device_id_type=pl.DeviceIdType.MESH
        )
    pl.semaphore_wait(barrier, len(greeted))

    def sends(source, step):
        to_left = pltpu.make_async_remote_copy(
            src_ref=source.at[pl.ds(0, pair)],
            dst_ref=halo.at[step, 1],
            send_sem=send_sem.at[step, 1],
            recv_sem=recv_sem.at[step, 1],
            device_id={"row": left},
            device_id_type=pl.DeviceIdType.MESH,
        )
        to_right = pltpu.make_async_remote_copy(
            src_ref=source.at[pl.ds(last, pair)],
            dst_ref=halo.at[step, 0],
            send_sem=send_sem.at[step, 0],
            recv_sem=recv_sem.at[step, 0],
            device_id={"row": right},
            device_id_type=pl.DeviceIdType.MESH,
        )
        return to_left, to_right

    copies = sends(start_ref, 0)
    for copy in copies:
        copy.start()

    def build(p, carry):
        for i in range(REACH):
            b = p * REACH + i
            live = (b < lengths_ref[0] - REACH) | (b >= block_count - REACH)
            places = []
            for t in range(tile_count):
                shift = lax.rem(
                    columns_ref[b * tile_count + t] - (me * block_count + b) + REACH + total_blocks,
                    total_blocks,
                )
                places.append(jnp.where(live, shift, -1))
            for c in range(3 * REACH):
                value = None
                if 0 <= c - i <= 2 * REACH:
                    for t in range(tile_count):
                        hit = jnp.where(places[t] == c - i, 1.0, 0.0).astype(jnp.float32)
                        mask = jnp.full((tile, tile), hit, jnp.float32).astype(jnp.bfloat16)
                        term = tiles_ref[b, t] * mask
                        value = term if value is None else value + term
                else:
                    value = jnp.zeros((tile, tile), jnp.bfloat16)
                band[p, i * tile : (i + 1) * tile, c * tile : (c + 1) * tile] = value
        return carry

    lax.fori_loop(0, pairs, build, 0)

    held = [start_ref] + [(odd, even)[step % 2] for step in range(CHEB - 1)] + [final]
    for step in range(CHEB):
        current, target = held[step], held[step + 1]
        earlier = held[step - 1] if step else None

        def finish(product, rows):
            if earlier is not None:
                product = 2.0 * product - earlier[rows, :].astype(jnp.float32)
            target[rows, :] = product.astype(jnp.bfloat16)

        for copy in copies:
            copy.wait()
        top = pl.ds(0, pair)
        finish(
            jnp.dot(band[0, :, :pair], halo[step, 0], preferred_element_type=jnp.float32)
            + jnp.dot(
                band[0, :, pair:], current[0 : 2 * pair, :], preferred_element_type=jnp.float32
            ),
            top,
        )
        finish(
            jnp.dot(
                band[pairs - 1, :, 2 * pair :], halo[step, 1], preferred_element_type=jnp.float32
            )
            + jnp.dot(
                band[pairs - 1, :, : 2 * pair],
                current[last - pair : last + pair, :],
                preferred_element_type=jnp.float32,
            ),
            pl.ds(last, pair),
        )

        def interior(p, carry):
            before = pl.multiple_of((p - 1) * pair, pair)
            here = pl.multiple_of(p * pair, pair)
            finish(
                jnp.dot(
                    band[p], current[pl.ds(before, 3 * pair), :], preferred_element_type=jnp.float32
                ),
                pl.ds(here, pair),
            )
            return carry

        if step < CHEB - 1:
            early = min(7, pairs - 1)
            lax.fori_loop(1, early, interior, 0, unroll=3)
            copies = sends(target, step + 1)
            for copy in copies:
                copy.start()
            lax.fori_loop(early, pairs - 1, interior, 0, unroll=4)

    def deliver(d):
        rows = share * pair
        source = final.at[pl.ds(pl.multiple_of(vec_at[d] * rows, pair), rows)]
        if d == 0:
            copy = pltpu.make_async_copy(source, out_ref.at[vec], keep_sem)
        else:
            copy = pltpu.make_async_remote_copy(
                src_ref=source,
                dst_ref=out_ref.at[vec],
                send_sem=panel_send.at[d - 1],
                recv_sem=panel_recv.at[d - 1],
                device_id={"vec": vec_at[d]},
                device_id_type=pl.DeviceIdType.MESH,
            )
        copy.start()
        return copy

    order = list(range(1, panels)) + [0]
    deliveries = []
    for n, d in enumerate(order):

        def quarter(p, carry):
            p = vec_at[d] * share + p
            p = p + lax.div(pairs - 1 - p, pairs - 1) - lax.div(p, pairs - 1)
            return interior(p, carry)

        lax.fori_loop(0, share, quarter, 0, unroll=4)
        if n:
            deliveries.append(deliver(order[n - 1]))
    deliveries.append(deliver(0))
    for copy in deliveries:
        copy.wait()


def chebyshev(ham_tiles, tile_columns, stack_lengths, start_vectors):
    block_count, tile_count, tile, _ = ham_tiles.shape
    rows, width = start_vectors.shape
    pair = REACH * tile
    panels = lax.axis_size("vec")
    vmem = pl.BlockSpec(memory_space=pltpu.VMEM)
    smem = pl.BlockSpec(memory_space=pltpu.SMEM)
    return pl.pallas_call(
        functools.partial(chebyshev_kernel, block_count * lax.axis_size("row")),
        out_shape=jax.ShapeDtypeStruct((panels, rows // panels, width), jnp.bfloat16),
        in_specs=[smem, smem, vmem, vmem],
        out_specs=pl.BlockSpec(memory_space=pltpu.HBM),
        scratch_shapes=[
            pltpu.VMEM((block_count // REACH, pair, 3 * pair), jnp.bfloat16),
            pltpu.VMEM((rows, width), jnp.bfloat16),
            pltpu.VMEM((rows, width), jnp.bfloat16),
            pltpu.VMEM((rows, width), jnp.bfloat16),
            pltpu.VMEM((CHEB, 2, pair, width), jnp.bfloat16),
            pltpu.SemaphoreType.DMA((CHEB, 2)),
            pltpu.SemaphoreType.DMA((CHEB, 2)),
            pltpu.SemaphoreType.DMA((panels - 1,)),
            pltpu.SemaphoreType.DMA((panels - 1,)),
            pltpu.SemaphoreType.DMA,
        ],
        compiler_params=pltpu.CompilerParams(
            collective_id=0, has_side_effects=True, vmem_limit_bytes=60 * 1024 * 1024
        ),
    )(tile_columns.reshape(-1), stack_lengths, ham_tiles, start_vectors)


def gram_sum_kernel(part_ref, out_ref, arrived, outgoing, total, near, thin, far, send_sem, recv_sem):
    _, quads, panels, _, _ = part_ref.shape
    row, vec = lax.axis_index("row"), lax.axis_index("vec")
    side, quad = lax.rem(row, 2), row // 2
    other = 1 - side
    partner = quad * 2 + other
    quad_at = [lax.rem(quad + d, quads) for d in range(quads)]
    vec_at = [lax.rem(vec + d, panels) for d in range(panels)]

    def ring(axis, places, make):
        copies = []
        for d in range(1, len(places)):
            source, target, slot = make(d)
            place = places[d] if axis == "vec" else places[d] * 2 + side
            copies.append(
                pltpu.make_async_remote_copy(
                    src_ref=source,
                    dst_ref=target,
                    send_sem=send_sem.at[slot],
                    recv_sem=recv_sem.at[slot],
                    device_id={axis: place},
                    device_id_type=pl.DeviceIdType.MESH,
                )
            )
        for copy in copies:
            copy.start()
        return copies

    def swap(source, target, slot):
        copy = pltpu.make_async_remote_copy(
            src_ref=source,
            dst_ref=target,
            send_sem=send_sem.at[slot],
            recv_sem=recv_sem.at[slot],
            device_id={"row": partner},
            device_id_type=pl.DeviceIdType.MESH,
        )
        copy.start()
        copy.wait()

    barrier = pltpu.get_barrier_semaphore()
    greeted = [{"row": partner}]
    greeted += [{"row": place * 2 + side} for place in quad_at[1:]]
    greeted += [{"vec": place} for place in vec_at[1:]]
    for device in greeted:
        pl.semaphore_signal(
            barrier, inc=1, device_id=device, device_id_type=pl.DeviceIdType.MESH
        )
    pl.semaphore_wait(barrier, len(greeted))

    slots = iter(range(2 + 2 * (quads - 1) + 2 * (panels - 1)))
    swap(part_ref.at[other], arrived, next(slots))
    for d in range(1, quads):
        place = quad_at[d]
        outgoing[place] = (part_ref[side, place] + arrived[place]).astype(jnp.bfloat16)
    total[...] = part_ref[side, quad] + arrived[quad]

    copies = ring(
        "row", quad_at, lambda d: (outgoing.at[quad_at[d]], near.at[d - 1], next(slots))
    )
    for d in range(1, quads):
        copies[d - 1].wait()
        total[...] += near[d - 1].astype(jnp.float32)

    thin[...] = total[...].astype(jnp.bfloat16)
    copies = ring("vec", vec_at, lambda d: (thin.at[vec_at[d]], far.at[d - 1], next(slots)))
    reduced = total[vec]
    for d in range(1, panels):
        copies[d - 1].wait()
        reduced += far[d - 1].astype(jnp.float32)
    out_ref[side, quad, vec] = reduced.astype(jnp.bfloat16)

    mine = out_ref.at[side, quad, vec]
    for copy in ring("vec", vec_at, lambda d: (mine, mine, next(slots))):
        copy.wait()
    mine = out_ref.at[side, quad]
    for copy in ring("row", quad_at, lambda d: (mine, mine, next(slots))):
        copy.wait()
    mine = out_ref.at[side]
    swap(mine, mine, next(slots))


def gram_sum(partial):
    rows, width = partial.shape
    quads, panels = lax.axis_size("row") // 2, lax.axis_size("vec")
    height = rows // (2 * quads * panels)
    copies = 2 + 2 * (quads - 1) + 2 * (panels - 1)
    vmem = pl.BlockSpec(memory_space=pltpu.VMEM)
    summed = pl.pallas_call(
        gram_sum_kernel,
        out_shape=jax.ShapeDtypeStruct((2, quads, panels, height, width), jnp.bfloat16),
        in_specs=[vmem],
        out_specs=vmem,
        scratch_shapes=[
            pltpu.VMEM((quads, panels, height, width), jnp.float32),
            pltpu.VMEM((quads, panels, height, width), jnp.bfloat16),
            pltpu.VMEM((panels, height, width), jnp.float32),
            pltpu.VMEM((quads - 1, panels, height, width), jnp.bfloat16),
            pltpu.VMEM((panels, height, width), jnp.bfloat16),
            pltpu.VMEM((panels - 1, height, width), jnp.bfloat16),
            pltpu.SemaphoreType.DMA((copies,)),
            pltpu.SemaphoreType.DMA((copies,)),
        ],
        compiler_params=pltpu.CompilerParams(
            collective_id=1, has_side_effects=True, vmem_limit_bytes=40 * 1024 * 1024
        ),
    )(partial.reshape(2, quads, panels, height, width))
    return summed.reshape(rows, width)


VMEM = pl.BlockSpec(memory_space=pltpu.VMEM)


def gram_parts_kernel(total_rows, panel_ref, out_ref):
    panels, _, width = panel_ref.shape
    n = 0
    for i in range(panels):
        for j in range(i + 1):
            product = lax.dot_general(
                panel_ref[j],
                panel_ref[i],
                (((0,), (0,)), ((), ())),
                preferred_element_type=jnp.float32,
            )
            out_ref[n * width : (n + 1) * width, :] = product / float(total_rows)
            n += 1
    tail = out_ref.shape[0] - n * width
    if tail:
        out_ref[n * width :, :] = jnp.zeros((tail, width), jnp.float32)


def gram_parts(panel_rows, total_rows):
    panels, _, width = panel_rows.shape
    unit = 16 * lax.axis_size("row") * panels
    rows = -(-(panels * (panels + 1) // 2 * width) // unit) * unit
    return pl.pallas_call(
        functools.partial(gram_parts_kernel, total_rows),
        out_shape=jax.ShapeDtypeStruct((rows, width), jnp.float32),
        in_specs=[VMEM],
        out_specs=VMEM,
        compiler_params=pltpu.CompilerParams(vmem_limit_bytes=40 * 1024 * 1024),
    )(panel_rows)


def weights_kernel(spectral_ref, packed_ref, out_ref, gram, high, low, side_high, side_low, base):
    panels, full, width = out_ref.shape
    diagonal = lax.broadcasted_iota(jnp.int32, (width, width), 0) == lax.broadcasted_iota(
        jnp.int32, (width, width), 1
    )
    trace = jnp.zeros((1, 1), jnp.float32)
    n = 0
    for i in range(panels):
        for j in range(i + 1):
            block = packed_ref[n * width : (n + 1) * width, :]
            n += 1
            gram[j * width : (j + 1) * width, i * width : (i + 1) * width] = block
            wide = block.astype(jnp.float32)
            if i == j:
                trace += jnp.sum(jnp.where(diagonal, wide, 0.0), axis=(0, 1), keepdims=True)
            else:
                gram[i * width : (i + 1) * width, j * width : (j + 1) * width] = wide.T.astype(
                    jnp.bfloat16
                )
    scale = spectral_ref[0] * trace / float(full)
    inverse = 1.0 / scale
    shrink = 1.0 / jnp.sqrt(scale)

    def squares(r, carry):
        rows = pl.ds(pl.multiple_of(r * width, width), width)
        square = jnp.dot(gram[rows, :], gram[...], preferred_element_type=jnp.float32)
        square = square * inverse * inverse
        system = gram[rows, :].astype(jnp.float32) * inverse
        top = square.astype(jnp.bfloat16)
        high[rows, :] = top
        low[rows, :] = (square - top.astype(jnp.float32)).astype(jnp.bfloat16)
        side = 0.0625 * square - 0.5625 * system
        top = side.astype(jnp.bfloat16)
        side_high[rows, :] = top
        side_low[rows, :] = (side - top.astype(jnp.float32)).astype(jnp.bfloat16)
        ones = lax.broadcasted_iota(jnp.int32, (width, full), 0) + r * width
        ones = ones == lax.broadcasted_iota(jnp.int32, (width, full), 1)
        base[rows, :] = (
            jnp.where(ones, 2.25, 0.0) - 2.4375 * system + 1.6875 * square
        )
        return carry

    lax.fori_loop(0, panels, squares, 0)

    def products(r, carry):
        rows = pl.ds(pl.multiple_of(r * width, width), width)
        product = (
            jnp.dot(high[rows, :], side_high[...], preferred_element_type=jnp.float32)
            + jnp.dot(high[rows, :], side_low[...], preferred_element_type=jnp.float32)
            + jnp.dot(low[rows, :], side_high[...], preferred_element_type=jnp.float32)
        )
        root = (base[rows, :] + product) * shrink
        for v in range(panels):
            out_ref[v, rows, :] = root[:, v * width : (v + 1) * width].astype(jnp.bfloat16)
        return carry

    lax.fori_loop(0, panels, products, 0)


def newton_schulz_weights(packed, spectral_scale, panels):
    width = packed.shape[1]
    full = panels * width
    return pl.pallas_call(
        weights_kernel,
        out_shape=jax.ShapeDtypeStruct((panels, full, width), jnp.bfloat16),
        in_specs=[pl.BlockSpec(memory_space=pltpu.SMEM), VMEM],
        out_specs=VMEM,
        scratch_shapes=[pltpu.VMEM((full, full), jnp.bfloat16)] * 5
        + [pltpu.VMEM((full, full), jnp.float32)],
        compiler_params=pltpu.CompilerParams(vmem_limit_bytes=50 * 1024 * 1024),
    )(spectral_scale, packed)


def basis_kernel(panel_ref, weights_ref, out_ref, result, send_sem, recv_sem, keep_sem):
    panels, rows, width = panel_ref.shape
    vec = lax.axis_index("vec")
    vec_at = [lax.rem(vec + d, panels) for d in range(panels)]
    barrier = pltpu.get_barrier_semaphore()
    for place in vec_at[1:]:
        pl.semaphore_signal(
            barrier, inc=1, device_id={"vec": place}, device_id_type=pl.DeviceIdType.MESH
        )
    pl.semaphore_wait(barrier, panels - 1)
    landing = out_ref.at[pl.ds(pl.multiple_of(vec * rows, rows), rows)]
    chunk = 256

    def deliver(d):
        source = result.at[vec_at[d]]
        if d == 0:
            copy = pltpu.make_async_copy(source, landing, keep_sem)
        else:
            copy = pltpu.make_async_remote_copy(
                src_ref=source,
                dst_ref=landing,
                send_sem=send_sem.at[d - 1],
                recv_sem=recv_sem.at[d - 1],
                device_id={"vec": vec_at[d]},
                device_id_type=pl.DeviceIdType.MESH,
            )
        copy.start()
        return copy

    order = list(range(1, panels)) + [0]
    deliveries = []
    for n, d in enumerate(order):

        def product(c, carry):
            here = pl.ds(pl.multiple_of(c * chunk, chunk), chunk)
            total = None
            for u in range(panels):
                term = jnp.dot(
                    panel_ref[u, here, :],
                    weights_ref[vec_at[d], u * width : (u + 1) * width, :],
                    preferred_element_type=jnp.float32,
                )
                total = term if total is None else total + term
            result[vec_at[d], here, :] = total.astype(jnp.bfloat16)
            return carry

        lax.fori_loop(0, rows // chunk, product, 0, unroll=2)
        if n:
            deliveries.append(deliver(order[n - 1]))
    deliveries.append(deliver(0))
    for copy in deliveries:
        copy.wait()


def basis(panel_rows, weights):
    panels, rows, width = panel_rows.shape
    return pl.pallas_call(
        basis_kernel,
        out_shape=jax.ShapeDtypeStruct((panels * rows, width), jnp.bfloat16),
        in_specs=[VMEM, VMEM],
        out_specs=pl.BlockSpec(memory_space=pltpu.HBM),
        scratch_shapes=[
            pltpu.VMEM((panels, rows, width), jnp.bfloat16),
            pltpu.SemaphoreType.DMA((panels - 1,)),
            pltpu.SemaphoreType.DMA((panels - 1,)),
            pltpu.SemaphoreType.DMA,
        ],
        compiler_params=pltpu.CompilerParams(
            collective_id=2, has_side_effects=True, vmem_limit_bytes=40 * 1024 * 1024
        ),
    )(panel_rows, weights)


def local(ham_tiles, tile_columns, stack_lengths, start_vectors, spectral_scale):
    total_rows = start_vectors.shape[0] * lax.axis_size("row")
    panel_rows = chebyshev(ham_tiles, tile_columns, stack_lengths, start_vectors)
    packed = gram_sum(gram_parts(panel_rows, total_rows))
    weights = newton_schulz_weights(packed, spectral_scale, lax.axis_size("vec"))
    return basis(panel_rows, weights)


def solution(mesh):
    placed = (P("row", None, None, None), P("row", None), P("row"), P("row", "vec"), P())
    return jax.shard_map(
        local, mesh=mesh, in_specs=placed, out_specs=P("row", "vec"), check_vma=False
    )
```

```python
import functools

import jax
import jax.numpy as jnp
from jax import lax
from jax.experimental import pallas as pl
from jax.experimental.pallas import tpu as pltpu
from jax.sharding import PartitionSpec as P

REACH = 2
CHEB = 6


def chebyshev_kernel(
    total_blocks,
    columns_ref,
    lengths_ref,
    tiles_ref,
    start_ref,
    out_ref,
    band,
    even,
    odd,
    final,
    halo,
    send_sem,
    recv_sem,
    panel_send,
    panel_recv,
    keep_sem,
):
    block_count, tile_count, tile, _ = tiles_ref.shape
    pair = REACH * tile
    pairs = block_count // REACH
    count = lax.axis_size("row")
    me = lax.axis_index("row")
    left, right = lax.rem(me + count - 1, count), lax.rem(me + 1, count)
    last = (pairs - 1) * pair
    vec, panels = lax.axis_index("vec"), lax.axis_size("vec")
    vec_at = [lax.rem(vec + d, panels) for d in range(panels)]
    share = pairs // panels

    barrier = pltpu.get_barrier_semaphore()
    greeted = [{"row": left}, {"row": right}] + [{"vec": place} for place in vec_at[1:]]
    for device in greeted:
        pl.semaphore_signal(
            barrier, inc=1, device_id=device, device_id_type=pl.DeviceIdType.MESH
        )
    pl.semaphore_wait(barrier, len(greeted))

    def sends(source, step):
        to_left = pltpu.make_async_remote_copy(
            src_ref=source.at[pl.ds(0, pair)],
            dst_ref=halo.at[step, 1],
            send_sem=send_sem.at[step, 1],
            recv_sem=recv_sem.at[step, 1],
            device_id={"row": left},
            device_id_type=pl.DeviceIdType.MESH,
        )
        to_right = pltpu.make_async_remote_copy(
            src_ref=source.at[pl.ds(last, pair)],
            dst_ref=halo.at[step, 0],
            send_sem=send_sem.at[step, 0],
            recv_sem=recv_sem.at[step, 0],
            device_id={"row": right},
            device_id_type=pl.DeviceIdType.MESH,
        )
        return to_left, to_right

    copies = sends(start_ref, 0)
    for copy in copies:
        copy.start()

    def build(p, carry):
        for i in range(REACH):
            b = p * REACH + i
            live = (b < lengths_ref[0] - REACH) | (b >= block_count - REACH)
            places = []
            for t in range(tile_count):
                shift = lax.rem(
                    columns_ref[b * tile_count + t] - (me * block_count + b) + REACH + total_blocks,
                    total_blocks,
                )
                places.append(jnp.where(live, shift, -1))
            for c in range(3 * REACH):
                value = None
                if 0 <= c - i <= 2 * REACH:
                    for t in range(tile_count):
                        hit = jnp.where(places[t] == c - i, 1.0, 0.0).astype(jnp.float32)
                        mask = jnp.full((tile, tile), hit, jnp.float32).astype(jnp.bfloat16)
                        term = tiles_ref[b, t] * mask
                        value = term if value is None else value + term
                else:
                    value = jnp.zeros((tile, tile), jnp.bfloat16)
                band[p, i * tile : (i + 1) * tile, c * tile : (c + 1) * tile] = value
        return carry

    lax.fori_loop(0, pairs, build, 0)

    held = [start_ref] + [(odd, even)[step % 2] for step in range(CHEB - 1)] + [final]

    def finish(step, product, rows):
        if step:
            product = 2.0 * product - held[step - 1][rows, :].astype(jnp.float32)
        held[step + 1][rows, :] = product.astype(jnp.bfloat16)

    def interior(step, p):
        before = pl.multiple_of((p - 1) * pair, pair)
        here = pl.multiple_of(p * pair, pair)
        finish(
            step,
            jnp.dot(
                band[p], held[step][pl.ds(before, 3 * pair), :], preferred_element_type=jnp.float32
            ),
            pl.ds(here, pair),
        )

    def deliver(d):
        rows = share * pair
        source = final.at[pl.ds(pl.multiple_of(vec_at[d] * rows, pair), rows)]
        if d == 0:
            return pltpu.make_async_copy(source, out_ref.at[vec], keep_sem)
        return pltpu.make_async_remote_copy(
            src_ref=source,
            dst_ref=out_ref.at[vec],
            send_sem=panel_send.at[d - 1],
            recv_sem=panel_recv.at[d - 1],
            device_id={"vec": vec_at[d]},
            device_id_type=pl.DeviceIdType.MESH,
        )

    order = list(range(1, panels)) + [0]
    deliveries = [deliver(d) for d in order]
    outer = panels // 4
    central = [(vec_at[d] >= outer) & (vec_at[d] < panels - outer) for d in order]

    edge = max(outer * share - CHEB + 1, 1)
    for step in range(CHEB):

        def centre(p, carry, step=step):
            interior(step, p)
            return carry

        lax.fori_loop(edge + step, pairs - edge - step, centre, 0, unroll=2)

    for step in range(CHEB):
        current = held[step]
        for copy in copies:
            copy.wait()
        finish(
            step,
            jnp.dot(band[0, :, :pair], halo[step, 0], preferred_element_type=jnp.float32)
            + jnp.dot(
                band[0, :, pair:], current[0 : 2 * pair, :], preferred_element_type=jnp.float32
            ),
            pl.ds(0, pair),
        )
        finish(
            step,
            jnp.dot(
                band[pairs - 1, :, 2 * pair :], halo[step, 1], preferred_element_type=jnp.float32
            )
            + jnp.dot(
                band[pairs - 1, :, : 2 * pair],
                current[last - pair : last + pair, :],
                preferred_element_type=jnp.float32,
            ),
            pl.ds(last, pair),
        )

        def sides(p, carry, step=step):
            interior(step, p)
            interior(step, pairs - 1 - p)
            return carry

        begin = min(2, edge + step)
        lax.fori_loop(1, begin, sides, 0)
        if step < CHEB - 1:
            copies = sends(held[step + 1], step + 1)
            for copy in copies:
                copy.start()
        if step == 0:
            for ready, copy in zip(central, deliveries):
                pl.when(ready)(copy.start)
        lax.fori_loop(begin, edge + step, sides, 0)

    for ready, copy in zip(central, deliveries):
        pl.when(jnp.logical_not(ready))(copy.start)
    for copy in deliveries:
        copy.wait()


def chebyshev(ham_tiles, tile_columns, stack_lengths, start_vectors):
    block_count, tile_count, tile, _ = ham_tiles.shape
    rows, width = start_vectors.shape
    pair = REACH * tile
    panels = lax.axis_size("vec")
    vmem = pl.BlockSpec(memory_space=pltpu.VMEM)
    smem = pl.BlockSpec(memory_space=pltpu.SMEM)
    return pl.pallas_call(
        functools.partial(chebyshev_kernel, block_count * lax.axis_size("row")),
        out_shape=jax.ShapeDtypeStruct((panels, rows // panels, width), jnp.bfloat16),
        in_specs=[smem, smem, vmem, vmem],
        out_specs=pl.BlockSpec(memory_space=pltpu.HBM),
        scratch_shapes=[
            pltpu.VMEM((block_count // REACH, pair, 3 * pair), jnp.bfloat16),
            pltpu.VMEM((rows, width), jnp.bfloat16),
            pltpu.VMEM((rows, width), jnp.bfloat16),
            pltpu.VMEM((rows, width), jnp.bfloat16),
            pltpu.VMEM((CHEB, 2, pair, width), jnp.bfloat16),
            pltpu.SemaphoreType.DMA((CHEB, 2)),
            pltpu.SemaphoreType.DMA((CHEB, 2)),
            pltpu.SemaphoreType.DMA((panels - 1,)),
            pltpu.SemaphoreType.DMA((panels - 1,)),
            pltpu.SemaphoreType.DMA,
        ],
        compiler_params=pltpu.CompilerParams(
            collective_id=0, has_side_effects=True, vmem_limit_bytes=60 * 1024 * 1024
        ),
    )(tile_columns.reshape(-1), stack_lengths, ham_tiles, start_vectors)


def gram_sum_kernel(part_ref, out_ref, arrived, outgoing, total, near, thin, far, send_sem, recv_sem):
    _, quads, panels, _, _ = part_ref.shape
    row, vec = lax.axis_index("row"), lax.axis_index("vec")
    side, quad = lax.rem(row, 2), row // 2
    other = 1 - side
    partner = quad * 2 + other
    quad_at = [lax.rem(quad + d, quads) for d in range(quads)]
    vec_at = [lax.rem(vec + d, panels) for d in range(panels)]

    def ring(axis, places, make):
        copies = []
        for d in range(1, len(places)):
            source, target, slot = make(d)
            place = places[d] if axis == "vec" else places[d] * 2 + side
            copies.append(
                pltpu.make_async_remote_copy(
                    src_ref=source,
                    dst_ref=target,
                    send_sem=send_sem.at[slot],
                    recv_sem=recv_sem.at[slot],
                    device_id={axis: place},
                    device_id_type=pl.DeviceIdType.MESH,
                )
            )
        for copy in copies:
            copy.start()
        return copies

    def swap(source, target, slot):
        copy = pltpu.make_async_remote_copy(
            src_ref=source,
            dst_ref=target,
            send_sem=send_sem.at[slot],
            recv_sem=recv_sem.at[slot],
            device_id={"row": partner},
            device_id_type=pl.DeviceIdType.MESH,
        )
        copy.start()
        copy.wait()

    barrier = pltpu.get_barrier_semaphore()
    greeted = [{"row": partner}]
    greeted += [{"row": place * 2 + side} for place in quad_at[1:]]
    greeted += [{"vec": place} for place in vec_at[1:]]
    for device in greeted:
        pl.semaphore_signal(
            barrier, inc=1, device_id=device, device_id_type=pl.DeviceIdType.MESH
        )
    pl.semaphore_wait(barrier, len(greeted))

    slots = iter(range(2 + 2 * (quads - 1) + 2 * (panels - 1)))
    swap(part_ref.at[other], arrived, next(slots))
    for d in range(1, quads):
        place = quad_at[d]
        outgoing[place] = (part_ref[side, place] + arrived[place]).astype(jnp.bfloat16)
    total[...] = part_ref[side, quad] + arrived[quad]

    copies = ring(
        "row", quad_at, lambda d: (outgoing.at[quad_at[d]], near.at[d - 1], next(slots))
    )
    for d in range(1, quads):
        copies[d - 1].wait()
        total[...] += near[d - 1].astype(jnp.float32)

    thin[...] = total[...].astype(jnp.bfloat16)
    copies = ring("vec", vec_at, lambda d: (thin.at[vec_at[d]], far.at[d - 1], next(slots)))
    reduced = total[vec]
    for d in range(1, panels):
        copies[d - 1].wait()
        reduced += far[d - 1].astype(jnp.float32)
    out_ref[side, quad, vec] = reduced.astype(jnp.bfloat16)

    mine = out_ref.at[side, quad, vec]
    for copy in ring("vec", vec_at, lambda d: (mine, mine, next(slots))):
        copy.wait()
    mine = out_ref.at[side, quad]
    for copy in ring("row", quad_at, lambda d: (mine, mine, next(slots))):
        copy.wait()
    mine = out_ref.at[side]
    swap(mine, mine, next(slots))


def gram_sum(partial):
    rows, width = partial.shape
    quads, panels = lax.axis_size("row") // 2, lax.axis_size("vec")
    height = rows // (2 * quads * panels)
    copies = 2 + 2 * (quads - 1) + 2 * (panels - 1)
    vmem = pl.BlockSpec(memory_space=pltpu.VMEM)
    summed = pl.pallas_call(
        gram_sum_kernel,
        out_shape=jax.ShapeDtypeStruct((2, quads, panels, height, width), jnp.bfloat16),
        in_specs=[vmem],
        out_specs=vmem,
        scratch_shapes=[
            pltpu.VMEM((quads, panels, height, width), jnp.float32),
            pltpu.VMEM((quads, panels, height, width), jnp.bfloat16),
            pltpu.VMEM((panels, height, width), jnp.float32),
            pltpu.VMEM((quads - 1, panels, height, width), jnp.bfloat16),
            pltpu.VMEM((panels, height, width), jnp.bfloat16),
            pltpu.VMEM((panels - 1, height, width), jnp.bfloat16),
            pltpu.SemaphoreType.DMA((copies,)),
            pltpu.SemaphoreType.DMA((copies,)),
        ],
        compiler_params=pltpu.CompilerParams(
            collective_id=1, has_side_effects=True, vmem_limit_bytes=40 * 1024 * 1024
        ),
    )(partial.reshape(2, quads, panels, height, width))
    return summed.reshape(rows, width)


VMEM = pl.BlockSpec(memory_space=pltpu.VMEM)


def gram_parts_kernel(total_rows, panel_ref, out_ref):
    panels, _, width = panel_ref.shape
    n = 0
    for i in range(panels):
        for j in range(i + 1):
            product = lax.dot_general(
                panel_ref[j],
                panel_ref[i],
                (((0,), (0,)), ((), ())),
                preferred_element_type=jnp.float32,
            )
            out_ref[n * width : (n + 1) * width, :] = product / float(total_rows)
            n += 1
    tail = out_ref.shape[0] - n * width
    if tail:
        out_ref[n * width :, :] = jnp.zeros((tail, width), jnp.float32)


def gram_parts(panel_rows, total_rows):
    panels, _, width = panel_rows.shape
    unit = 16 * lax.axis_size("row") * panels
    rows = -(-(panels * (panels + 1) // 2 * width) // unit) * unit
    return pl.pallas_call(
        functools.partial(gram_parts_kernel, total_rows),
        out_shape=jax.ShapeDtypeStruct((rows, width), jnp.float32),
        in_specs=[VMEM],
        out_specs=VMEM,
        compiler_params=pltpu.CompilerParams(vmem_limit_bytes=40 * 1024 * 1024),
    )(panel_rows)


def weights_kernel(spectral_ref, packed_ref, out_ref, gram, high, low, side_high, side_low, base):
    panels, full, width = out_ref.shape
    diagonal = lax.broadcasted_iota(jnp.int32, (width, width), 0) == lax.broadcasted_iota(
        jnp.int32, (width, width), 1
    )
    trace = jnp.zeros((1, 1), jnp.float32)
    n = 0
    for i in range(panels):
        for j in range(i + 1):
            block = packed_ref[n * width : (n + 1) * width, :]
            n += 1
            gram[j * width : (j + 1) * width, i * width : (i + 1) * width] = block
            wide = block.astype(jnp.float32)
            if i == j:
                trace += jnp.sum(jnp.where(diagonal, wide, 0.0), axis=(0, 1), keepdims=True)
            else:
                gram[i * width : (i + 1) * width, j * width : (j + 1) * width] = wide.T.astype(
                    jnp.bfloat16
                )
    scale = spectral_ref[0] * trace / float(full)
    inverse = 1.0 / scale
    shrink = 1.0 / jnp.sqrt(scale)

    def squares(r, carry):
        rows = pl.ds(pl.multiple_of(r * width, width), width)
        square = jnp.dot(gram[rows, :], gram[...], preferred_element_type=jnp.float32)
        square = square * inverse * inverse
        system = gram[rows, :].astype(jnp.float32) * inverse
        top = square.astype(jnp.bfloat16)
        high[rows, :] = top
        low[rows, :] = (square - top.astype(jnp.float32)).astype(jnp.bfloat16)
        side = 0.0625 * square - 0.5625 * system
        top = side.astype(jnp.bfloat16)
        side_high[rows, :] = top
        side_low[rows, :] = (side - top.astype(jnp.float32)).astype(jnp.bfloat16)
        ones = lax.broadcasted_iota(jnp.int32, (width, full), 0) + r * width
        ones = ones == lax.broadcasted_iota(jnp.int32, (width, full), 1)
        base[rows, :] = (
            jnp.where(ones, 2.25, 0.0) - 2.4375 * system + 1.6875 * square
        )
        return carry

    lax.fori_loop(0, panels, squares, 0)

    def products(r, carry):
        rows = pl.ds(pl.multiple_of(r * width, width), width)
        product = (
            jnp.dot(high[rows, :], side_high[...], preferred_element_type=jnp.float32)
            + jnp.dot(high[rows, :], side_low[...], preferred_element_type=jnp.float32)
            + jnp.dot(low[rows, :], side_high[...], preferred_element_type=jnp.float32)
        )
        root = (base[rows, :] + product) * shrink
        for v in range(panels):
            out_ref[v, rows, :] = root[:, v * width : (v + 1) * width].astype(jnp.bfloat16)
        return carry

    lax.fori_loop(0, panels, products, 0)


def newton_schulz_weights(packed, spectral_scale, panels):
    width = packed.shape[1]
    full = panels * width
    return pl.pallas_call(
        weights_kernel,
        out_shape=jax.ShapeDtypeStruct((panels, full, width), jnp.bfloat16),
        in_specs=[pl.BlockSpec(memory_space=pltpu.SMEM), VMEM],
        out_specs=VMEM,
        scratch_shapes=[pltpu.VMEM((full, full), jnp.bfloat16)] * 5
        + [pltpu.VMEM((full, full), jnp.float32)],
        compiler_params=pltpu.CompilerParams(vmem_limit_bytes=50 * 1024 * 1024),
    )(spectral_scale, packed)


def basis_kernel(panel_ref, weights_ref, out_ref, result, send_sem, recv_sem, keep_sem):
    panels, rows, width = panel_ref.shape
    vec = lax.axis_index("vec")
    vec_at = [lax.rem(vec + d, panels) for d in range(panels)]
    barrier = pltpu.get_barrier_semaphore()
    for place in vec_at[1:]:
        pl.semaphore_signal(
            barrier, inc=1, device_id={"vec": place}, device_id_type=pl.DeviceIdType.MESH
        )
    pl.semaphore_wait(barrier, panels - 1)
    landing = out_ref.at[pl.ds(pl.multiple_of(vec * rows, rows), rows)]
    chunk = 256

    def deliver(d):
        source = result.at[vec_at[d]]
        if d == 0:
            copy = pltpu.make_async_copy(source, landing, keep_sem)
        else:
            copy = pltpu.make_async_remote_copy(
                src_ref=source,
                dst_ref=landing,
                send_sem=send_sem.at[d - 1],
                recv_sem=recv_sem.at[d - 1],
                device_id={"vec": vec_at[d]},
                device_id_type=pl.DeviceIdType.MESH,
            )
        copy.start()
        return copy

    order = list(range(1, panels)) + [0]
    deliveries = []
    for n, d in enumerate(order):

        def product(c, carry):
            here = pl.ds(pl.multiple_of(c * chunk, chunk), chunk)
            total = None
            for u in range(panels):
                term = jnp.dot(
                    panel_ref[u, here, :],
                    weights_ref[vec_at[d], u * width : (u + 1) * width, :],
                    preferred_element_type=jnp.float32,
                )
                total = term if total is None else total + term
            result[vec_at[d], here, :] = total.astype(jnp.bfloat16)
            return carry

        lax.fori_loop(0, rows // chunk, product, 0, unroll=2)
        if n:
            deliveries.append(deliver(order[n - 1]))
    deliveries.append(deliver(0))
    for copy in deliveries:
        copy.wait()


def basis(panel_rows, weights):
    panels, rows, width = panel_rows.shape
    return pl.pallas_call(
        basis_kernel,
        out_shape=jax.ShapeDtypeStruct((panels * rows, width), jnp.bfloat16),
        in_specs=[VMEM, VMEM],
        out_specs=pl.BlockSpec(memory_space=pltpu.HBM),
        scratch_shapes=[
            pltpu.VMEM((panels, rows, width), jnp.bfloat16),
            pltpu.SemaphoreType.DMA((panels - 1,)),
            pltpu.SemaphoreType.DMA((panels - 1,)),
            pltpu.SemaphoreType.DMA,
        ],
        compiler_params=pltpu.CompilerParams(
            collective_id=2, has_side_effects=True, vmem_limit_bytes=40 * 1024 * 1024
        ),
    )(panel_rows, weights)


def local(ham_tiles, tile_columns, stack_lengths, start_vectors, spectral_scale):
    total_rows = start_vectors.shape[0] * lax.axis_size("row")
    panel_rows = chebyshev(ham_tiles, tile_columns, stack_lengths, start_vectors)
    packed = gram_sum(gram_parts(panel_rows, total_rows))
    weights = newton_schulz_weights(packed, spectral_scale, lax.axis_size("vec"))
    return basis(panel_rows, weights)


def solution(mesh):
    placed = (P("row", None, None, None), P("row", None), P("row"), P("row", "vec"), P())
    return jax.shard_map(
        local, mesh=mesh, in_specs=placed, out_specs=P("row", "vec"), check_vma=False
    )
```
